128 devices in a mesh: str: 32 (over x, z, y_hi), chol: 4 (over y_lo, core).
Axes of the slice: x: 4, y: 4 (y_hi: 2, y_lo: 2; y = y_hi * 2 + y_lo), z: 4, core: 2. Of those that a mesh axis runs over, the one named last changes fastest.
Arguments:
- amplitudes: bfloat16 [4, 4096, 4096], P(None, 'str'), may hold values from -6 to 6
- alpha_values: bfloat16 [4, 32, 8, 128, 128], P('chol'), may hold values from -0.1875 to 0.1875
- alpha_cols: int32 [4, 32, 8], P('chol'), may hold values from 0 to 31, all different within a row
- beta_values: bfloat16 [4, 32, 8, 128, 128], P('chol'), may hold values from -0.1875 to 0.1875
- beta_cols: int32 [4, 32, 8], P('chol'), may hold values from 0 to 31, all different within a row
Outputs:
- sigma: float32 [4, 4096, 4096], P(None, 'chol', 'str')
The draws below stay inside these ranges and needn't reach their ends.
Inputs may be any that keep to these rules, and one draw needn't show every extreme that they name: `alpha_cols`: within one block row the 8 block columns are distinct. `beta_cols`: within one block row the 8 block columns are distinct.
All inputs are finite; a program needn't handle non-finite values.
Results may differ from the reference program's by a relative error of at most 0.0029.
Values may be sent and summed in bfloat16 or wider, within the bound.
No kernel may reach another device: no remote copies, remote signals or barrier semaphores. Data moves between devices by JAX's collectives and lax.ppermute only.
A program may use at most 128 MiB of HBM per device.

```python
import jax
import jax.numpy as jnp
from jax import lax

BLK = 128
NNZ = 8
R = 4
NA = 4096
NB = 4096
NBLK = 32
K = 4


def block_scale(rng, shape, pieces, smallest, high):
    gain = 1.0
    for axis_at, blocks in pieces:
        heights = jax.random.uniform(jax.random.fold_in(jax.random.fold_in(rng, 6), axis_at), (blocks,), jnp.float32, smallest / len(pieces), high / len(pieces))
        gain = gain * jnp.repeat(jnp.exp(heights), shape[axis_at] // blocks).reshape((-1,) + (1,) * (len(shape) - 1 - axis_at))
    return gain


def choose_distinct(key, rows, number_of, top, lift):
    order = jax.random.permutation(jax.random.fold_in(key, 1), number_of)
    pull = order
    for power in range(3):
        pull = pull * pull // number_of
    pull = pull * lift // number_of
    tickets = jax.random.randint(jax.random.fold_in(key, 2), (rows, number_of), 0, 4096) + pull
    fixed_rows = jax.random.permutation(jax.random.fold_in(key, 3), rows)[jnp.arange(number_of) % rows]
    tickets = jnp.where(jnp.arange(rows)[:, None] == fixed_rows[None, :], 1 << 14, tickets)
    score = tickets * number_of + jnp.arange(number_of)
    return lax.top_k(score.astype(jnp.int32), top)[1].astype(jnp.int32)


def gaussian(key, shape, scale, bound, split=(), held_as=jnp.bfloat16):
    factor_of = block_scale(key, shape, split, -0.22, 0.18) if split else 1.0
    drawn = jax.random.normal(key, shape, jnp.float32) * scale * factor_of
    return jnp.minimum(jnp.maximum(drawn, -bound), bound).astype(held_as)


def setup_inputs(seed: int = 0) -> dict:
    seeds = jax.random.split(jax.random.key(seed), 6)
    amplitudes = gaussian(seeds[0], (R, NA, NB), 1.0, 6.0, ((1, 32),))
    alpha_values = gaussian(seeds[1], (K, NBLK, NNZ, BLK, BLK), (NNZ * BLK) ** -0.5, 0.1875, ((0, 4),))
    alpha_cols = choose_distinct(seeds[2], K * NBLK, NBLK, NNZ, 0).reshape((K, NBLK, NNZ))
    beta_values = gaussian(seeds[3], (K, NBLK, NNZ, BLK, BLK), (NNZ * BLK) ** -0.5, 0.1875, ((0, 4),))
    beta_cols = choose_distinct(seeds[4], K * NBLK, NBLK, NNZ, 0).reshape((K, NBLK, NNZ))
    return {"amplitudes": amplitudes, "alpha_values": alpha_values, "alpha_cols": alpha_cols, "beta_values": beta_values, "beta_cols": beta_cols}


def beta_side(amplitudes, values, cols):
    nvec, na, nb = amplitudes.shape
    blk = values.shape[-1]
    nblk = nb // blk
    blocks = amplitudes.reshape(nvec, na, nblk, blk)

    def one_row(j):
        picked = jnp.take(blocks, cols[j], axis=2).astype(jnp.float32)
        return jnp.einsum('ramc,mdc->rad', picked, values[j].astype(jnp.float32))

    parts = lax.map(one_row, jnp.arange(nblk, dtype=jnp.int32))
    return jnp.transpose(parts, (1, 2, 0, 3)).reshape(nvec, na, nb).astype(jnp.bfloat16)


def alpha_side(half, values, cols):
    nvec, na, nb = half.shape
    blk = values.shape[-1]
    nblk = na // blk
    blocks = half.reshape(nvec, nblk, blk, nb)

    def one_row(i):
        picked = jnp.take(blocks, cols[i], axis=1).astype(jnp.float32)
        return jnp.einsum('rmcq,mdc->rdq', picked, values[i].astype(jnp.float32))

    parts = lax.map(one_row, jnp.arange(nblk, dtype=jnp.int32))
    return jnp.transpose(parts, (1, 0, 2, 3)).reshape(nvec, na, nb)


def reference(amplitudes, alpha_values, alpha_cols, beta_values, beta_cols):
    total = jnp.zeros(amplitudes.shape, jnp.float32)
    for vector in range(K):
        half = beta_side(amplitudes, beta_values[vector], beta_cols[vector])
        total = total + alpha_side(half, alpha_values[vector], alpha_cols[vector])
    return total
```

```python
import functools

import jax
import jax.numpy as jnp
from jax import lax
from jax.experimental import pallas as pl
from jax.experimental.pallas import tpu as pltpu
from jax.sharding import PartitionSpec as P

CHUNKS = 1
J = 4
VMEM_LIMIT = 56 << 20


def beta_kernel(cols_ref, a_ref, v_ref, o_ref):
    nvec, rows, _ = a_ref.shape
    per_step, nnz, blk, _ = v_ref.shape
    g = pl.program_id(0)
    for jj in range(per_step):
        picked = []
        for m in range(nnz):
            at = pl.multiple_of(cols_ref[g * per_step + jj, m] * blk, blk)
            picked.append(a_ref[:, :, pl.ds(at, blk)].reshape(nvec * rows, blk))
        lhs = jnp.concatenate(picked, axis=1)
        rhs = jnp.concatenate([v_ref[jj, m] for m in range(nnz)], axis=1)
        acc = lax.dot_general(lhs, rhs, (((1,), (1,)), ((), ())), preferred_element_type=jnp.float32)
        o_ref[jj] = acc.reshape(nvec, rows, blk).astype(o_ref.dtype)


def beta_side(amplitudes, values, cols):
    nvec, rows, width = amplitudes.shape
    nblk, nnz, blk, _ = values.shape
    return pl.pallas_call(
        beta_kernel,
        grid_spec=pltpu.PrefetchScalarGridSpec(
            num_scalar_prefetch=1,
            grid=(nblk // J,),
            in_specs=[
                pl.BlockSpec((nvec, rows, width), lambda g, c: (0, 0, 0)),
                pl.BlockSpec((J, nnz, blk, blk), lambda g, c: (g, 0, 0, 0)),
            ],
            out_specs=pl.BlockSpec((J, nvec, rows, blk), lambda g, c: (g, 0, 0, 0)),
        ),
        out_shape=jax.ShapeDtypeStruct((nblk, nvec, rows, blk), jnp.bfloat16),
        cost_estimate=pl.CostEstimate(
            flops=2 * nvec * rows * nblk * nnz * blk * blk,
            bytes_accessed=2 * (amplitudes.size + values.size + nblk * nvec * rows * blk),
            transcendentals=0,
        ),
        compiler_params=pltpu.CompilerParams(vmem_limit_bytes=VMEM_LIMIT),
        name="beta_side",
    )(cols, amplitudes, values)


def alpha_kernel(order_ref, cols_ref, h_ref, v_ref, send_ref, keep_ref):
    _, nvec, blk, width = h_ref.shape
    per_step, nnz, _, _ = v_ref.shape
    g = pl.program_id(0)
    half_way = pl.num_programs(0) // 2
    base = order_ref[g] * per_step
    for ii in range(per_step):
        lhs = jnp.concatenate([v_ref[ii, m] for m in range(nnz)], axis=1)
        rhs = []
        for r in range(nvec):
            rhs.append(
                jnp.concatenate([h_ref[cols_ref[base + ii, m], r] for m in range(nnz)], axis=0)
            )
        rhs = jnp.concatenate(rhs, axis=1)
        acc = lax.dot_general(lhs, rhs, (((1,), (0,)), ((), ())), preferred_element_type=jnp.float32)

        @pl.when(g < half_way)
        def _():
            for r in range(nvec):
                send_ref[r, ii * blk : (ii + 1) * blk] = acc[:, r * width : (r + 1) * width].astype(send_ref.dtype)

        @pl.when(g >= half_way)
        def _():
            for r in range(nvec):
                keep_ref[r, ii * blk : (ii + 1) * blk] = acc[:, r * width : (r + 1) * width]


def alpha_side(half, values, cols, order):
    nblk, nvec, blk, width = half.shape
    nnz = values.shape[1]
    steps = nblk // J
    per_dest = steps // 4
    half_way = steps // 2

    def piece(step):
        return (step // per_dest, 0, step % per_dest, 0)

    rows = nblk * blk // 4
    return pl.pallas_call(
        alpha_kernel,
        grid_spec=pltpu.PrefetchScalarGridSpec(
            num_scalar_prefetch=2,
            grid=(steps,),
            in_specs=[
                pl.BlockSpec((nblk, nvec, blk, width), lambda g, o, c: (0, 0, 0, 0)),
                pl.BlockSpec((J, nnz, blk, blk), lambda g, o, c: (o[g], 0, 0, 0)),
            ],
            out_specs=[
                pl.BlockSpec((None, nvec, J * blk, width), lambda g, o, c: piece(jnp.minimum(g, half_way - 1))),
                pl.BlockSpec((None, nvec, J * blk, width), lambda g, o, c: piece(jnp.maximum(g - half_way, 0))),
            ],
        ),
        out_shape=[
            jax.ShapeDtypeStruct((2, nvec, rows, width), jnp.bfloat16),
            jax.ShapeDtypeStruct((2, nvec, rows, width), jnp.float32),
        ],
        cost_estimate=pl.CostEstimate(
            flops=2 * nvec * width * nblk * nnz * blk * blk,
            bytes_accessed=2 * (half.size + values.size) + 3 * nvec * nblk * blk * width,
            transcendentals=0,
        ),
        compiler_params=pltpu.CompilerParams(vmem_limit_bytes=VMEM_LIMIT),
        name="alpha_side",
    )(order, cols, half, values)


def flipped(bit):
    return [(c, c ^ bit) for c in range(4)]


def body(amplitudes, alpha_values, alpha_cols, beta_values, beta_cols):
    nvec = amplitudes.shape[0]
    steps = alpha_values.shape[1] // J
    per_dest = steps // 4
    me = lax.axis_index("chol")
    rel = jnp.repeat(jnp.array([3, 1, 2, 0], jnp.int32), per_dest)
    order = (me ^ rel) * per_dest + jnp.arange(steps, dtype=jnp.int32) % per_dest
    size = nvec // CHUNKS
    outs = []
    for q in range(CHUNKS):
        half = beta_side(amplitudes[q * size : (q + 1) * size], beta_values[0], beta_cols[0])
        moved = lax.all_to_all(half, "str", split_axis=0, concat_axis=0, tiled=True)
        send, keep = alpha_side(moved, alpha_values[0], alpha_cols[0], order)
        got = lax.ppermute(send, "chol", flipped(1))
        both = keep + got.astype(jnp.float32)
        far = lax.ppermute(both[0].astype(jnp.bfloat16), "chol", flipped(2))
        outs.append(both[1] + far.astype(jnp.float32))
    return jnp.concatenate(outs, axis=0)


def solution(mesh):
    placed = (
        P(None, "str", None),
        P("chol", None, None, None, None),
        P("chol", None, None),
        P("chol", None, None, None, None),
        P("chol", None, None),
    )
    return jax.shard_map(
        body, mesh=mesh, in_specs=placed, out_specs=P(None, "chol", "str"), check_vma=False
    )
```

```python
import jax
import jax.numpy as jnp
from jax import lax
from jax.experimental import pallas as pl
from jax.experimental.pallas import tpu as pltpu
from jax.sharding import PartitionSpec as P


CHOL = 4
GROUP = 4
BETA_LIMIT = 57 << 20
ALPHA_LIMIT = 12 << 20
SMALL = 8 << 20
STAY = pl.BlockSpec(memory_space=pl.ANY)


def beta_side(cols, values, amplitudes):
    nvec, rows, width = amplitudes.shape
    nblk, nnz, blk, _ = values.shape

    def kernel(cols_ref, v_ref, a_ref, o_ref, a_buf, v_buf, o_buf, a_sem, v_sem, o_sem):
        def a_copy(r):
            return pltpu.make_async_copy(a_ref.at[r], a_buf.at[r], a_sem.at[r])

        def v_copy(g):
            part = pl.ds(g * GROUP, GROUP)
            return pltpu.make_async_copy(v_ref.at[part], v_buf.at[part], v_sem.at[g])

        def o_copy(g):
            part = pl.ds(g * GROUP, GROUP)
            return pltpu.make_async_copy(o_buf.at[part], o_ref.at[part], o_sem.at[g])

        for r in range(nvec):
            a_copy(r).start()
        for g in range(nblk // GROUP):
            v_copy(g).start()
        for r in range(nvec):
            a_copy(r).wait()

        @pl.loop(0, nblk // GROUP)
        def _(g):
            v_copy(g).wait()
            for n in range(GROUP):
                t = g * GROUP + n
                picked = []
                for m in range(nnz):
                    col = pl.multiple_of(cols_ref[m, t] * blk, blk)
                    picked.append(a_buf[:, :, pl.ds(col, blk)].reshape(nvec * rows, blk))
                lhs = jnp.concatenate(picked, axis=1)
                rhs = jnp.concatenate([v_buf[t, m] for m in range(nnz)], axis=1)
                acc = lax.dot_general(lhs, rhs, (((1,), (1,)), ((), ())), preferred_element_type=jnp.float32)
                o_buf[t] = acc.reshape(nvec, rows, blk).astype(o_buf.dtype)
            o_copy(g).start()

        for g in range(nblk // GROUP):
            o_copy(g).wait()

    out = (nblk, nvec, rows, blk)
    return pl.pallas_call(
        kernel,
        grid_spec=pltpu.PrefetchScalarGridSpec(
            num_scalar_prefetch=1,
            grid=(),
            in_specs=[STAY, STAY],
            out_specs=STAY,
            scratch_shapes=[
                pltpu.VMEM((nvec, rows, width), jnp.bfloat16),
                pltpu.VMEM(values.shape, jnp.bfloat16),
                pltpu.VMEM(out, jnp.bfloat16),
                pltpu.SemaphoreType.DMA((nvec,)),
                pltpu.SemaphoreType.DMA((nblk // GROUP,)),
                pltpu.SemaphoreType.DMA((nblk // GROUP,)),
            ],
        ),
        out_shape=jax.ShapeDtypeStruct(out, jnp.bfloat16),
        cost_estimate=pl.CostEstimate(
            flops=4 * nvec * rows * nblk * nnz * blk * blk,
            bytes_accessed=2 * (amplitudes.size + values.size + nvec * nblk * rows * blk),
            transcendentals=0,
        ),
        compiler_params=pltpu.CompilerParams(vmem_limit_bytes=BETA_LIMIT),
        name="beta_side",
    )(cols, values, amplitudes)


def alpha_side(me, cols, values, half, first, nvec, rel, dtype, addend=None):
    nblk, nnz, blk, _ = values.shape
    width = half.shape[-1]
    per = nblk // CHOL

    def kernel(me_ref, cols_ref, v_ref, h_ref, *rest):
        extra, (o_ref, v_buf, v_sem) = rest[:-3], rest[-3:]
        base = (me_ref[0] ^ rel) * per

        def v_copy(g):
            src = v_ref.at[pl.ds(base + g * GROUP, GROUP)]
            return pltpu.make_async_copy(src, v_buf.at[pl.ds(g * GROUP, GROUP)], v_sem.at[g])

        for g in range(per // GROUP):
            v_copy(g).start()
        for g in range(per // GROUP):
            v_copy(g).wait()
            for n in range(g * GROUP, (g + 1) * GROUP):
                lhs = jnp.concatenate([v_buf[n, m] for m in range(nnz)], axis=1)
                spots = [cols_ref[m, base + n] for m in range(nnz)]
                rhs = jnp.concatenate(
                    [jnp.concatenate([h_ref[s, first + r] for s in spots], axis=0) for r in range(nvec)], axis=1
                )
                acc = lax.dot_general(lhs, rhs, (((1,), (0,)), ((), ())), preferred_element_type=jnp.float32)
                rows = slice(n * blk, (n + 1) * blk)
                for r in range(nvec):
                    term = acc[:, r * width : (r + 1) * width]
                    if extra:
                        term = term + extra[0][r, rows].astype(jnp.float32)
                    o_ref[r, rows] = term.astype(o_ref.dtype)

    out = (nvec, per * blk, width)
    inside = pl.BlockSpec(memory_space=pltpu.VMEM)
    return pl.pallas_call(
        kernel,
        grid_spec=pltpu.PrefetchScalarGridSpec(
            num_scalar_prefetch=2,
            grid=(),
            in_specs=[STAY, inside] + [inside] * (addend is not None),
            out_specs=inside,
            scratch_shapes=[
                pltpu.VMEM((per, nnz, blk, blk), jnp.bfloat16),
                pltpu.SemaphoreType.DMA((per // GROUP,)),
            ],
        ),
        out_shape=jax.ShapeDtypeStruct(out, dtype),
        cost_estimate=pl.CostEstimate(
            flops=2 * nvec * width * per * nnz * blk * blk,
            bytes_accessed=2 * half.size + 2 * per * nnz * blk * blk,
            transcendentals=0,
        ),
        compiler_params=pltpu.CompilerParams(vmem_limit_bytes=ALPHA_LIMIT),
        name="alpha_side",
    )(me, cols, values, half, *([addend] if addend is not None else []))


def finish(own, parts):
    total, rows, width = own.shape
    cut = 2
    out, first = None, 0
    for away in parts:
        nvec = away.shape[0]

        def kernel(own_ref, away_ref, *rest):
            rest[-1][...] = own_ref[...] + away_ref[...].astype(jnp.float32)

        spec = pl.BlockSpec((nvec, rows // cut, width), lambda g: (0, g, 0))
        part = pl.BlockSpec((nvec, rows // cut, width), lambda g, at=first // nvec: (at, g, 0))
        out = pl.pallas_call(
            kernel,
            grid=(cut,),
            in_specs=[part, spec] + [pl.BlockSpec(memory_space=pl.ANY)] * (out is not None),
            out_specs=part,
            out_shape=jax.ShapeDtypeStruct((total, rows, width), jnp.float32),
            input_output_aliases={2: 0} if out is not None else {},
            compiler_params=pltpu.CompilerParams(vmem_limit_bytes=SMALL),
            name="finish",
        )(own, away, *([out] if out is not None else []))
        first += nvec
    return out


def swap(value, bits):
    return lax.ppermute(value, "chol", [(c, c ^ bits) for c in range(CHOL)])


def body(amplitudes, alpha_values, alpha_cols, beta_values, beta_cols):
    nvec = amplitudes.shape[0]
    me = lax.axis_index("chol").astype(jnp.int32).reshape(1)
    av, bv = alpha_values[0], beta_values[0]
    ac = jnp.swapaxes(alpha_cols[0], 0, 1)
    bc = jnp.swapaxes(beta_cols[0], 0, 1)
    bf16, f32 = jnp.bfloat16, jnp.float32
    size = nvec // 2
    me, ac, bc = lax.optimization_barrier((me, ac, bc))
    half = beta_side(bc, bv, amplitudes)
    half = lax.all_to_all(half, "str", split_axis=0, concat_axis=0, tiled=True)
    far, away = [], []
    for n in range(2):
        far.append(swap(alpha_side(me, ac, av, half, n * size, size, 3, bf16), 1))
    for n in range(2):
        near = alpha_side(me, ac, av, half, n * size, size, 2, bf16, far[n])
        away.append(swap(near, 2))
    side = swap(alpha_side(me, ac, av, half, 0, nvec, 1, bf16), 1)
    rest = alpha_side(me, ac, av, half, 0, nvec, 0, f32, side)
    return finish(rest, away)


def solution(mesh):
    placed = (
        P(None, "str", None),
        P("chol", None, None, None, None),
        P("chol", None, None),
        P("chol", None, None, None, None),
        P("chol", None, None),
    )
    return jax.shard_map(
        body, mesh=mesh, in_specs=placed, out_specs=P(None, "chol", "str"), check_vma=False
    )
```

```python
import jax
import jax.numpy as jnp
from jax import lax
from jax.experimental import pallas as pl
from jax.experimental.pallas import tpu as pltpu
from jax.sharding import PartitionSpec as P


CHOL = 4
GROUP = 8
SIZES = (2, 2)
PASSES = 1
AHEAD = 2
CUT = 2
BETA_LIMIT = 57 << 20
ALPHA_LIMIT = 12 << 20
SMALL = 8 << 20
STAY = pl.BlockSpec(memory_space=pl.ANY)


def beta_side(cols, values, amplitudes):
    nvec, rows, width = amplitudes.shape
    nblk, nnz, blk, _ = values.shape
    groups = nblk // GROUP
    size = nvec // PASSES

    def kernel(cols_ref, v_ref, a_ref, o_ref, a_buf, v_buf, o_buf, a_sem, v_sem, o_sem):
        def a_copy(p):
            part = pl.ds(p * size, size)
            return pltpu.make_async_copy(a_ref.at[part], a_buf.at[part], a_sem.at[p])

        def v_copy(g):
            part = pl.ds(g * GROUP, GROUP)
            return pltpu.make_async_copy(v_ref.at[part], v_buf.at[part], v_sem.at[g])

        def o_copy(p, g):
            part = (pl.ds(g * GROUP, GROUP), pl.ds(p * size, size))
            return pltpu.make_async_copy(o_buf.at[part], o_ref.at[part], o_sem.at[p, g])

        v_copy(0).start()
        a_copy(0).start()
        for g in range(1, AHEAD):
            v_copy(g).start()
        for p in range(PASSES):
            a_copy(p).wait()

            @pl.loop(0, groups)
            def _(g):
                if p == 0:

                    @pl.when(g + AHEAD < groups)
                    def _():
                        v_copy(g + AHEAD).start()

                    if PASSES > 1:

                        @pl.when(g < PASSES - 1)
                        def _():
                            a_copy(g + 1).start()

                    v_copy(g).wait()
                for n in range(GROUP):
                    t = g * GROUP + n
                    picked = []
                    for m in range(nnz):
                        col = pl.multiple_of(cols_ref[m, t] * blk, blk)
                        picked.append(a_buf[p * size : (p + 1) * size, :, pl.ds(col, blk)].reshape(size * rows, blk))
                    lhs = jnp.concatenate(picked, axis=1)
                    rhs = jnp.concatenate([v_buf[t, m] for m in range(nnz)], axis=1)
                    acc = lax.dot_general(lhs, rhs, (((1,), (1,)), ((), ())), preferred_element_type=jnp.float32)
                    o_buf[t, p * size : (p + 1) * size] = acc.reshape(size, rows, blk).astype(o_buf.dtype)
                o_copy(p, g).start()

        for p in range(PASSES):
            for g in range(groups):
                o_copy(p, g).wait()

    out = (nblk, nvec, rows, blk)
    return pl.pallas_call(
        kernel,
        grid_spec=pltpu.PrefetchScalarGridSpec(
            num_scalar_prefetch=1,
            grid=(),
            in_specs=[STAY, STAY],
            out_specs=STAY,
            scratch_shapes=[
                pltpu.VMEM((nvec, rows, width), jnp.bfloat16),
                pltpu.VMEM(values.shape, jnp.bfloat16),
                pltpu.VMEM(out, jnp.bfloat16),
                pltpu.SemaphoreType.DMA((PASSES,)),
                pltpu.SemaphoreType.DMA((groups,)),
                pltpu.SemaphoreType.DMA((PASSES, groups)),
            ],
        ),
        out_shape=jax.ShapeDtypeStruct(out, jnp.bfloat16),
        cost_estimate=pl.CostEstimate(
            flops=4 * nvec * rows * nblk * nnz * blk * blk,
            bytes_accessed=2 * (amplitudes.size + values.size + nvec * nblk * rows * blk),
            transcendentals=0,
        ),
        compiler_params=pltpu.CompilerParams(vmem_limit_bytes=BETA_LIMIT),
        name="beta_side",
    )(cols, values, amplitudes)


def alpha_side(me, cols, values, half, first, nvec, rel, dtype, addend=None):
    nblk, nnz, blk, _ = values.shape
    width = half.shape[-1]
    per = nblk // CHOL

    def kernel(me_ref, cols_ref, v_ref, h_ref, *rest):
        extra, o_ref = rest[:-1], rest[-1]
        base = (me_ref[0] ^ rel) * per
        for n in range(per):
            lhs = jnp.concatenate([v_ref[base + n, m] for m in range(nnz)], axis=1)
            spots = [cols_ref[m, base + n] for m in range(nnz)]
            rhs = jnp.concatenate(
                [jnp.concatenate([h_ref[s, first + r] for s in spots], axis=0) for r in range(nvec)], axis=1
            )
            acc = lax.dot_general(lhs, rhs, (((1,), (0,)), ((), ())), preferred_element_type=jnp.float32)
            rows = slice(n * blk, (n + 1) * blk)
            for r in range(nvec):
                term = acc[:, r * width : (r + 1) * width]
                if extra:
                    term = term + extra[0][r, rows].astype(jnp.float32)
                o_ref[r, rows] = term.astype(o_ref.dtype)

    out = (nvec, per * blk, width)
    inside = pl.BlockSpec(memory_space=pltpu.VMEM)
    return pl.pallas_call(
        kernel,
        grid_spec=pltpu.PrefetchScalarGridSpec(
            num_scalar_prefetch=2,
            grid=(),
            in_specs=[inside] * (2 + (addend is not None)),
            out_specs=inside,
        ),
        out_shape=jax.ShapeDtypeStruct(out, dtype),
        cost_estimate=pl.CostEstimate(
            flops=2 * nvec * width * per * nnz * blk * blk,
            bytes_accessed=2 * half.size + 2 * per * nnz * blk * blk,
            transcendentals=0,
        ),
        compiler_params=pltpu.CompilerParams(vmem_limit_bytes=ALPHA_LIMIT),
        name="alpha_side",
    )(me, cols, values, half, *([addend] if addend is not None else []))


def finish(own, parts):
    total, rows, width = own.shape
    out, first = None, 0
    for away in parts:
        nvec = away.shape[0]

        def kernel(own_ref, away_ref, *rest):
            rest[-1][...] = own_ref[...] + away_ref[...].astype(jnp.float32)

        spec = pl.BlockSpec((nvec, rows // CUT, width), lambda g: (0, g, 0))
        part = pl.BlockSpec(
            (pl.Element(nvec), pl.Element(rows // CUT), pl.Element(width)),
            lambda g, first=first: (first, g * (rows // CUT), 0),
        )
        out = pl.pallas_call(
            kernel,
            grid=(CUT,),
            in_specs=[part, spec] + [pl.BlockSpec(memory_space=pl.ANY)] * (out is not None),
            out_specs=part,
            out_shape=jax.ShapeDtypeStruct((total, rows, width), jnp.float32),
            input_output_aliases={2: 0} if out is not None else {},
            compiler_params=pltpu.CompilerParams(vmem_limit_bytes=SMALL),
            name="finish",
        )(own, away, *([out] if out is not None else []))
        first += nvec
    return out


def swap(value, bits):
    return lax.ppermute(value, "chol", [(c, c ^ bits) for c in range(CHOL)])


def body(amplitudes, alpha_values, alpha_cols, beta_values, beta_cols):
    nvec = amplitudes.shape[0]
    me = lax.axis_index("chol").astype(jnp.int32).reshape(1)
    av, bv = alpha_values[0], beta_values[0]
    ac = jnp.swapaxes(alpha_cols[0], 0, 1)
    bc = jnp.swapaxes(beta_cols[0], 0, 1)
    bf16, f32 = jnp.bfloat16, jnp.float32
    firsts = [sum(SIZES[:n]) for n in range(len(SIZES))]
    me, ac, bc = lax.optimization_barrier((me, ac, bc))
    half = beta_side(bc, bv, amplitudes)
    half = lax.all_to_all(half, "str", split_axis=0, concat_axis=0, tiled=True)
    far, away = [], []
    for n, size in enumerate(SIZES):
        far.append(swap(alpha_side(me, ac, av, half, firsts[n], size, 3, bf16), 1))
    for n, size in enumerate(SIZES):
        near = alpha_side(me, ac, av, half, firsts[n], size, 2, bf16, far[n])
        away.append(swap(near, 2))
    side = swap(alpha_side(me, ac, av, half, 0, nvec, 1, bf16), 1)
    rest = alpha_side(me, ac, av, half, 0, nvec, 0, f32, side)
    return finish(rest, away)


def solution(mesh):
    placed = (
        P(None, "str", None),
        P("chol", None, None, None, None),
        P("chol", None, None),
        P("chol", None, None, None, None),
        P("chol", None, None),
    )
    return jax.shard_map(
        body, mesh=mesh, in_specs=placed, out_specs=P(None, "chol", "str"), check_vma=False
    )
```

```python
import jax
import jax.numpy as jnp
from jax import lax
from jax.experimental import pallas as pl
from jax.experimental.pallas import tpu as pltpu
from jax.sharding import PartitionSpec as P


CHOL = 4
GROUP = 16
SIZES = (2, 2)
AHEAD = 1
CUT = 2
BETA_LIMIT = 57 << 20
ALPHA_LIMIT = 12 << 20
SMALL = 8 << 20
STAY = pl.BlockSpec(memory_space=pl.ANY)


def beta_side(cols, values, amplitudes):
    nvec, rows, _ = amplitudes.shape
    nblk, nnz, blk, _ = values.shape
    groups = nblk // GROUP

    def kernel(cols_ref, v_ref, a_ref, o_ref, a_buf, t_buf, v_buf, o_buf, a_sem, v_sem, o_sem):
        def a_copy(c):
            src = a_ref.at[:, :, pl.ds(pl.multiple_of(c * blk, blk), blk)]
            return pltpu.make_async_copy(src, a_buf.at[c], a_sem.at[c])

        def v_copy(g):
            part = pl.ds(g * GROUP, GROUP)
            return pltpu.make_async_copy(v_ref.at[part], v_buf.at[part], v_sem.at[g])

        def o_copy(g):
            part = pl.ds(g * GROUP, GROUP)
            return pltpu.make_async_copy(o_buf.at[part], o_ref.at[part], o_sem.at[g])

        for c in range(nblk):
            a_copy(c).start()
        for g in range(AHEAD):
            v_copy(g).start()

        @pl.loop(0, nblk // GROUP)
        def _(g):
            for n in range(GROUP):
                c = g * GROUP + n
                a_copy(c).wait()
                for r in range(nvec):
                    t_buf[c, :, r * rows : (r + 1) * rows] = jnp.transpose(a_buf[c, r])

        @pl.loop(0, groups)
        def _(g):
            @pl.when(g + AHEAD < groups)
            def _():
                v_copy(g + AHEAD).start()

            v_copy(g).wait()
            for n in range(GROUP):
                t = g * GROUP + n
                lhs = jnp.concatenate([v_buf[t, m] for m in range(nnz)], axis=1)
                rhs = jnp.concatenate([t_buf[cols_ref[m, t]] for m in range(nnz)], axis=0)
                acc = lax.dot_general(lhs, rhs, (((1,), (0,)), ((), ())), preferred_element_type=jnp.float32)
                for r in range(nvec):
                    o_buf[t, r] = jnp.transpose(acc[:, r * rows : (r + 1) * rows].astype(o_buf.dtype))
            o_copy(g).start()

        for g in range(groups):
            o_copy(g).wait()

    out = (nblk, nvec, rows, blk)
    return pl.pallas_call(
        kernel,
        grid_spec=pltpu.PrefetchScalarGridSpec(
            num_scalar_prefetch=1,
            grid=(),
            in_specs=[STAY, STAY],
            out_specs=STAY,
            scratch_shapes=[
                pltpu.VMEM((nblk, nvec, rows, blk), jnp.bfloat16),
                pltpu.VMEM((nblk, blk, nvec * rows), jnp.bfloat16),
                pltpu.VMEM(values.shape, jnp.bfloat16),
                pltpu.VMEM(out, jnp.bfloat16),
                pltpu.SemaphoreType.DMA((nblk,)),
                pltpu.SemaphoreType.DMA((groups,)),
                pltpu.SemaphoreType.DMA((groups,)),
            ],
        ),
        out_shape=jax.ShapeDtypeStruct(out, jnp.bfloat16),
        cost_estimate=pl.CostEstimate(
            flops=4 * nvec * rows * nblk * nnz * blk * blk,
            bytes_accessed=2 * (amplitudes.size + values.size + nvec * nblk * rows * blk),
            transcendentals=0,
        ),
        compiler_params=pltpu.CompilerParams(vmem_limit_bytes=BETA_LIMIT),
        name="beta_side",
    )(cols, values, amplitudes)


def alpha_side(me, cols, values, half, first, nvec, rel, dtype, addend=None):
    nblk, nnz, blk, _ = values.shape
    width = half.shape[-1]
    per = nblk // CHOL

    def kernel(me_ref, cols_ref, v_ref, h_ref, *rest):
        extra, o_ref = rest[:-1], rest[-1]
        base = (me_ref[0] ^ rel) * per
        for n in range(per):
            lhs = jnp.concatenate([v_ref[base + n, m] for m in range(nnz)], axis=1)
            spots = [cols_ref[m, base + n] for m in range(nnz)]
            rhs = jnp.concatenate(
                [jnp.concatenate([h_ref[s, first + r] for s in spots], axis=0) for r in range(nvec)], axis=1
            )
            acc = lax.dot_general(lhs, rhs, (((1,), (0,)), ((), ())), preferred_element_type=jnp.float32)
            rows = slice(n * blk, (n + 1) * blk)
            for r in range(nvec):
                term = acc[:, r * width : (r + 1) * width]
                if extra:
                    term = term + extra[0][r, rows].astype(jnp.float32)
                o_ref[r, rows] = term.astype(o_ref.dtype)

    out = (nvec, per * blk, width)
    inside = pl.BlockSpec(memory_space=pltpu.VMEM)
    return pl.pallas_call(
        kernel,
        grid_spec=pltpu.PrefetchScalarGridSpec(
            num_scalar_prefetch=2,
            grid=(),
            in_specs=[inside] * (2 + (addend is not None)),
            out_specs=inside,
        ),
        out_shape=jax.ShapeDtypeStruct(out, dtype),
        cost_estimate=pl.CostEstimate(
            flops=2 * nvec * width * per * nnz * blk * blk,
            bytes_accessed=2 * half.size + 2 * per * nnz * blk * blk,
            transcendentals=0,
        ),
        compiler_params=pltpu.CompilerParams(vmem_limit_bytes=ALPHA_LIMIT),
        name="alpha_side",
    )(me, cols, values, half, *([addend] if addend is not None else []))


def finish(own, parts):
    total, rows, width = own.shape
    out, first = None, 0
    for away in parts:
        nvec = away.shape[0]

        def kernel(own_ref, away_ref, *rest):
            rest[-1][...] = own_ref[...] + away_ref[...].astype(jnp.float32)

        spec = pl.BlockSpec((nvec, rows // CUT, width), lambda g: (0, g, 0))
        part = pl.BlockSpec(
            (pl.Element(nvec), pl.Element(rows // CUT), pl.Element(width)),
            lambda g, first=first: (first, g * (rows // CUT), 0),
        )
        out = pl.pallas_call(
            kernel,
            grid=(CUT,),
            in_specs=[part, spec] + [pl.BlockSpec(memory_space=pl.ANY)] * (out is not None),
            out_specs=part,
            out_shape=jax.ShapeDtypeStruct((total, rows, width), jnp.float32),
            input_output_aliases={2: 0} if out is not None else {},
            compiler_params=pltpu.CompilerParams(vmem_limit_bytes=SMALL),
            name="finish",
        )(own, away, *([out] if out is not None else []))
        first += nvec
    return out


def swap(value, bits):
    return lax.ppermute(value, "chol", [(c, c ^ bits) for c in range(CHOL)])


def body(amplitudes, alpha_values, alpha_cols, beta_values, beta_cols):
    nvec = amplitudes.shape[0]
    me = lax.axis_index("chol").astype(jnp.int32).reshape(1)
    av, bv = alpha_values[0], beta_values[0]
    ac = jnp.swapaxes(alpha_cols[0], 0, 1)
    bc = jnp.swapaxes(beta_cols[0], 0, 1)
    bf16, f32 = jnp.bfloat16, jnp.float32
    firsts = [sum(SIZES[:n]) for n in range(len(SIZES))]
    me, ac, bc = lax.optimization_barrier((me, ac, bc))
    half = beta_side(bc, bv, amplitudes)
    half = lax.all_to_all(half, "str", split_axis=0, concat_axis=0, tiled=True)
    far, away = [], []
    for n, size in enumerate(SIZES):
        far.append(swap(alpha_side(me, ac, av, half, firsts[n], size, 3, bf16), 1))
    for n, size in enumerate(SIZES):
        near = alpha_side(me, ac, av, half, firsts[n], size, 2, bf16, far[n])
        away.append(swap(near, 2))
    side = swap(alpha_side(me, ac, av, half, 0, nvec, 1, bf16), 1)
    rest = alpha_side(me, ac, av, half, 0, nvec, 0, f32, side)
    return finish(rest, away)


def solution(mesh):
    placed = (
        P(None, "str", None),
        P("chol", None, None, None, None),
        P("chol", None, None),
        P("chol", None, None, None, None),
        P("chol", None, None),
    )
    return jax.shard_map(
        body, mesh=mesh, in_specs=placed, out_specs=P(None, "chol", "str"), check_vma=False
    )
```

```python
import jax
import jax.numpy as jnp
from jax import lax
from jax.experimental import pallas as pl
from jax.experimental.pallas import tpu as pltpu
from jax.sharding import PartitionSpec as P


CHOL = 4
GROUP = 16
SIZES = (2, 2)
AHEAD = 1
CUT = 1
BETA_LIMIT = 57 << 20
ALPHA_LIMIT = 12 << 20
SMALL = 8 << 20
STAY = pl.BlockSpec(memory_space=pl.ANY)


def beta_side(cols, values, amplitudes):
    nvec, rows, _ = amplitudes.shape
    nblk, nnz, blk, _ = values.shape
    groups = nblk // GROUP

    def kernel(cols_ref, v_ref, a_ref, o_ref, a_buf, t_buf, v_buf, o_buf, a_sem, v_sem, o_sem):
        def a_copy(c):
            src = a_ref.at[:, :, pl.ds(pl.multiple_of(c * blk, blk), blk)]
            return pltpu.make_async_copy(src, a_buf.at[c], a_sem.at[c])

        def v_copy(g):
            part = pl.ds(g * GROUP, GROUP)
            return pltpu.make_async_copy(v_ref.at[part], v_buf.at[part], v_sem.at[g])

        def o_copy(g):
            part = pl.ds(g * GROUP, GROUP)
            return pltpu.make_async_copy(o_buf.at[part], o_ref.at[part], o_sem.at[g])

        for c in range(nblk):
            a_copy(c).start()
        for g in range(AHEAD):
            v_copy(g).start()

        @pl.loop(0, nblk // 8)
        def _(g):
            for n in range(8):
                a_copy(g * 8 + n).wait()
            for n in range(8):
                c = g * 8 + n
                for r in range(nvec):
                    t_buf[c, :, r * rows : (r + 1) * rows] = jnp.transpose(a_buf[c, r])

        @pl.loop(0, groups)
        def _(g):
            @pl.when(g + AHEAD < groups)
            def _():
                v_copy(g + AHEAD).start()

            v_copy(g).wait()
            for n in range(GROUP):
                t = g * GROUP + n
                lhs = jnp.concatenate([v_buf[t, m] for m in range(nnz)], axis=1)
                rhs = jnp.concatenate([t_buf[cols_ref[m, t]] for m in range(nnz)], axis=0)
                acc = lax.dot_general(lhs, rhs, (((1,), (0,)), ((), ())), preferred_element_type=jnp.float32)
                for r in range(nvec):
                    o_buf[t, r] = jnp.transpose(acc[:, r * rows : (r + 1) * rows].astype(o_buf.dtype))
            o_copy(g).start()

        for g in range(groups):
            o_copy(g).wait()

    out = (nblk, nvec, rows, blk)
    return pl.pallas_call(
        kernel,
        grid_spec=pltpu.PrefetchScalarGridSpec(
            num_scalar_prefetch=1,
            grid=(),
            in_specs=[STAY, STAY],
            out_specs=STAY,
            scratch_shapes=[
                pltpu.VMEM((nblk, nvec, rows, blk), jnp.bfloat16),
                pltpu.VMEM((nblk, blk, nvec * rows), jnp.bfloat16),
                pltpu.VMEM(values.shape, jnp.bfloat16),
                pltpu.VMEM(out, jnp.bfloat16),
                pltpu.SemaphoreType.DMA((nblk,)),
                pltpu.SemaphoreType.DMA((groups,)),
                pltpu.SemaphoreType.DMA((groups,)),
            ],
        ),
        out_shape=jax.ShapeDtypeStruct(out, jnp.bfloat16),
        cost_estimate=pl.CostEstimate(
            flops=4 * nvec * rows * nblk * nnz * blk * blk,
            bytes_accessed=2 * (amplitudes.size + values.size + nvec * nblk * rows * blk),
            transcendentals=0,
        ),
        compiler_params=pltpu.CompilerParams(vmem_limit_bytes=BETA_LIMIT),
        name="beta_side",
    )(cols, values, amplitudes)


def alpha_side(me, cols, values, half, first, nvec, rel, dtype, addend=None):
    nblk, nnz, blk, _ = values.shape
    width = half.shape[-1]
    per = nblk // CHOL

    def kernel(me_ref, cols_ref, v_ref, h_ref, *rest):
        extra, o_ref = rest[:-1], rest[-1]
        base = (me_ref[0] ^ rel) * per
        for n in range(per):
            lhs = jnp.concatenate([v_ref[base + n, m] for m in range(nnz)], axis=1)
            spots = [cols_ref[m, base + n] for m in range(nnz)]
            rhs = jnp.concatenate(
                [jnp.concatenate([h_ref[s, first + r] for s in spots], axis=0) for r in range(nvec)], axis=1
            )
            acc = lax.dot_general(lhs, rhs, (((1,), (0,)), ((), ())), preferred_element_type=jnp.float32)
            rows = slice(n * blk, (n + 1) * blk)
            for r in range(nvec):
                term = acc[:, r * width : (r + 1) * width]
                if extra:
                    term = term + extra[0][r, rows].astype(jnp.float32)
                o_ref[r, rows] = term.astype(o_ref.dtype)

    out = (nvec, per * blk, width)
    inside = pl.BlockSpec(memory_space=pltpu.VMEM)
    return pl.pallas_call(
        kernel,
        grid_spec=pltpu.PrefetchScalarGridSpec(
            num_scalar_prefetch=2,
            grid=(),
            in_specs=[inside] * (2 + (addend is not None)),
            out_specs=inside,
        ),
        out_shape=jax.ShapeDtypeStruct(out, dtype),
        cost_estimate=pl.CostEstimate(
            flops=2 * nvec * width * per * nnz * blk * blk,
            bytes_accessed=2 * half.size + 2 * per * nnz * blk * blk,
            transcendentals=0,
        ),
        compiler_params=pltpu.CompilerParams(vmem_limit_bytes=ALPHA_LIMIT),
        name="alpha_side",
    )(me, cols, values, half, *([addend] if addend is not None else []))


def finish(own, parts):
    total, rows, width = own.shape
    out, first = None, 0
    for away in parts:
        nvec = away.shape[0]

        def kernel(own_ref, away_ref, *rest):
            rest[-1][...] = own_ref[...] + away_ref[...].astype(jnp.float32)

        spec = pl.BlockSpec((nvec, rows // CUT, width), lambda g: (0, g, 0))
        part = pl.BlockSpec(
            (pl.Element(nvec), pl.Element(rows // CUT), pl.Element(width)),
            lambda g, first=first: (first, g * (rows // CUT), 0),
        )
        out = pl.pallas_call(
            kernel,
            grid=(CUT,),
            in_specs=[part, spec] + [pl.BlockSpec(memory_space=pl.ANY)] * (out is not None),
            out_specs=part,
            out_shape=jax.ShapeDtypeStruct((total, rows, width), jnp.float32),
            input_output_aliases={2: 0} if out is not None else {},
            compiler_params=pltpu.CompilerParams(vmem_limit_bytes=SMALL),
            name="finish",
        )(own, away, *([out] if out is not None else []))
        first += nvec
    return out


def swap(value, bits):
    return lax.ppermute(value, "chol", [(c, c ^ bits) for c in range(CHOL)])


def body(amplitudes, alpha_values, alpha_cols, beta_values, beta_cols):
    nvec = amplitudes.shape[0]
    me = lax.axis_index("chol").astype(jnp.int32).reshape(1)
    av, bv = alpha_values[0], beta_values[0]
    ac = jnp.swapaxes(alpha_cols[0], 0, 1)
    bc = jnp.swapaxes(beta_cols[0], 0, 1)
    bf16, f32 = jnp.bfloat16, jnp.float32
    firsts = [sum(SIZES[:n]) for n in range(len(SIZES))]
    me, ac, bc = lax.optimization_barrier((me, ac, bc))
    half = beta_side(bc, bv, amplitudes)
    half = lax.all_to_all(half, "str", split_axis=0, concat_axis=0, tiled=True)
    far, away = [], []
    for n, size in enumerate(SIZES):
        far.append(swap(alpha_side(me, ac, av, half, firsts[n], size, 3, bf16), 1))
    for n, size in enumerate(SIZES):
        near = alpha_side(me, ac, av, half, firsts[n], size, 2, bf16, far[n])
        away.append(swap(near, 2))
    side = swap(alpha_side(me, ac, av, half, 0, nvec, 1, bf16), 1)
    rest = alpha_side(me, ac, av, half, 0, nvec, 0, f32, side)
    return finish(rest, away)


def solution(mesh):
    placed = (
        P(None, "str", None),
        P("chol", None, None, None, None),
        P("chol", None, None),
        P("chol", None, None, None, None),
        P("chol", None, None),
    )
    return jax.shard_map(
        body, mesh=mesh, in_specs=placed, out_specs=P(None, "chol", "str"), check_vma=False
    )
```
